512 devices in a mesh: space: 64 (over y_hi, z, core), snap: 8 (over x, y_lo).
Axes of the slice: x: 4, y: 4 (y_hi: 2, y_lo: 2; y = y_hi * 2 + y_lo), z: 16, core: 2. Of those that a mesh axis runs over, the one named last changes fastest.
Arguments:
- snaps_primal: bfloat16 [2048, 196608], P('snap', 'space'), may hold values from -6 to 6
- snaps_adjoint: bfloat16 [2048, 196608], P('snap', 'space'), may hold values from -6 to 6
- coef_primal: bfloat16 [2048, 256], P('snap'), may hold values from -0.1875 to 0.1875
- coef_adjoint: bfloat16 [2048, 256], P('snap'), may hold values from -0.1875 to 0.1875
- op_blocks: bfloat16 [1536, 5, 128, 128], P('space'), may hold values from -0.25 to 0.25
- counts: int32 [1536], P('space'), may hold values from 1 to 5, as said below
- col_index: int32 [1536, 5], P('space'), may hold values from 0 to 47, as said below
- ghost_send: int32 [64, 4, 6], P('space'), may hold values from 0 to 23, as said below
Outputs:
- primal_modes: bfloat16 [256, 196608], P('snap', 'space')
- applied: bfloat16 [256, 196608], P('snap', 'space')
- reduced_operator: float32 [256, 256], P(None, 'snap')
- cross_gram: float32 [256, 256], P(None, 'snap')
The draws below stay inside these ranges and needn't reach their ends.
Inputs may be any that keep to these rules, and one draw needn't show every extreme that they name: `counts`: every block row has its slot 0 live. `col_index`: slot 0 of every block row names the row's own diagonal block; ghost entries never name a partition outside 0 to 63. `ghost_send`: the 6 entries of one list are distinct.
All inputs are finite; a program needn't handle non-finite values.
Results may differ from the reference program's by a relative error of at most 0.02.
Values may be sent and summed in bfloat16 or wider, within the bound.
No kernel may reach another device: no remote copies, remote signals or barrier semaphores. Data moves between devices by JAX's collectives and lax.ppermute only.
A program may use at most 64 MiB of HBM per device.

```python
import math
import jax
import jax.numpy as jnp
from jax import lax

R = 256
BS = 128
NBL = 24
KMAX = 5
GH = 6
M = 2048
NPART = 64
NSP = 196608
NBT = 1536
N_SNAP = 8


def draw_counts(key, part):
    values = jax.random.randint(key, (NBT,), 1, KMAX + 1)
    rows = jnp.arange(NBT, dtype=jnp.int32)
    values = jnp.where(rows % NBL == 0, jnp.maximum(values, 3), values)
    values = values.at[0].set(KMAX).at[1].set(1)
    return values.astype(jnp.int32)


def draw_col_index(key, part):
    extent = NBL + 4 * GH
    slots = jax.random.randint(jax.random.fold_in(key, 7), (NBT, KMAX), 0, extent)
    rows = jnp.arange(NBT, dtype=jnp.int32)
    owner = rows // NBL
    direction = jnp.clip((slots - NBL) // GH, 0, 3)
    offsets = jnp.array([-2, -1, 1, 2], dtype=jnp.int32)
    source = owner[:, None] + offsets[direction]
    inside = (source >= 0) & (source < NPART)
    slots = jnp.where((slots >= NBL) & jnp.logical_not(inside), slots % NBL, slots)
    slots = slots.at[:, 0].set(rows % NBL)
    first_rows = (rows % NBL == 0) & (owner + 2 < NPART)
    slots = slots.at[:, 1].set(jnp.where(first_rows, extent - 1, slots[:, 1]))
    low_rows = (rows % NBL == 0) & (owner >= 2)
    slots = slots.at[:, 2].set(jnp.where(low_rows, NBL, slots[:, 2]))
    middle = NPART // 2 * NBL
    slots = slots.at[middle, 1].set(extent - 1)
    slots = slots.at[0, 1].set(NBL + 2 * GH).at[0, 2].set(NBL + 3 * GH)
    return slots.astype(jnp.int32)


def draw_ghost_send(key, part):
    keys = jax.random.split(jax.random.fold_in(key, 11), NPART * 4)
    lists = jax.vmap(lambda single: jax.random.permutation(single, NBL)[:GH])(keys)
    lists = lists.reshape(NPART, 4, GH)
    steps_up = jnp.arange(GH, dtype=jnp.int32)
    lists = lists.at[0, 0].set(steps_up).at[0, 1].set(NBL - 1 - steps_up)
    return lists.astype(jnp.int32)


def with_spikes(entries, key, source, target, shards_of, factor):
    def block_of(axis_at):
        return (jnp.arange(entries.shape[axis_at]) // (entries.shape[axis_at] // shards_of)).reshape((-1,) + (1,) * (entries.ndim - 1 - axis_at))

    first = jax.random.permutation(key, shards_of)[block_of(target)]
    other_side = (block_of(target) + shards_of // 2) % shards_of
    return jnp.where((block_of(source) == first) | (block_of(source) == other_side), factor * entries, entries)


def steps_of(key, shape, shards, least, high):
    def one(position, blocks):
        heights = jax.random.uniform(jax.random.fold_in(jax.random.fold_in(key, 6), position), (blocks,), jnp.float32, least / len(shards), high / len(shards))
        return jnp.repeat(jnp.exp(heights), shape[position] // blocks).reshape((-1,) + (1,) * (len(shape) - position - 1))

    level = one(*shards[0])
    for cut in shards[1:]:
        level = level * one(*cut)
    return level


def normal_values(stream_key, shape, deviation, reach, pieces=(), held_as=jnp.bfloat16):
    gain = steps_of(stream_key, shape, pieces, -0.22, 0.18) if pieces else 1.0
    values = jax.random.normal(stream_key, shape, jnp.float32) * deviation * gain
    return jnp.minimum(jnp.maximum(values, -reach), reach).astype(held_as)


def heavy_noise(rng, shape, scale, limit, cuts, heavy, held_as=jnp.bfloat16):
    drawn = scale * jax.random.normal(rng, shape, jnp.float32)
    if cuts:
        drawn = drawn * steps_of(rng, shape, cuts, -0.22, 0.18)
    return jnp.clip(with_spikes(drawn, jax.random.fold_in(rng, 3), *heavy), -limit, limit).astype(held_as)


def setup_inputs(seed: int = 0) -> dict:
    seeds = jax.random.split(jax.random.key(seed), 9)
    return {
        "snaps_primal": normal_values(seeds[0], (M, NSP), 1.0, 6.0, ((0, 8), (1, 64))),
        "snaps_adjoint": normal_values(seeds[1], (M, NSP), 1.0, 6.0, ((0, 8), (1, 64))),
        "coef_primal": heavy_noise(seeds[2], (M, R), M ** -0.5, 0.1875, ((0, 8),), (0, 1, 8, 2.0)),
        "coef_adjoint": heavy_noise(seeds[3], (M, R), M ** -0.5, 0.1875, ((0, 8),), (0, 1, 8, 2.0)),
        "op_blocks": normal_values(seeds[4], (NBT, KMAX, BS, BS), (BS * KMAX) ** -0.5, 0.25, ((0, 64),)),
        "counts": draw_counts(jax.random.fold_in(seeds[8], 71), 0),
        "col_index": draw_col_index(jax.random.fold_in(seeds[8], 71), 0),
        "ghost_send": draw_ghost_send(jax.random.fold_in(seeds[8], 71), 0),
    }


def make_modes(snaps, coef):
    width = M // N_SNAP
    total = jnp.zeros((R, NSP), jnp.float32)
    for group in range(N_SNAP):
        partial_term = jnp.dot(coef[group * width:(group + 1) * width].T, snaps[group * width:(group + 1) * width], preferred_element_type=jnp.float32)
        rounded = lax.optimization_barrier(partial_term.astype(jnp.bfloat16))
        total = total + rounded.astype(jnp.float32)
    return total.astype(jnp.bfloat16)

def reference(snaps_primal, snaps_adjoint, coef_primal, coef_adjoint, op_blocks, counts, col_index, ghost_send):
    primal = make_modes(snaps_primal, coef_primal)
    adjoint = make_modes(snaps_adjoint, coef_adjoint)
    rows = jnp.arange(NBT, dtype=jnp.int32)
    owner = rows // NBL
    ghost = col_index >= NBL
    direction = jnp.clip((col_index - NBL) // GH, 0, 3).astype(jnp.int32)
    entry = ((col_index - NBL) % GH).astype(jnp.int32)
    offsets = jnp.array([-2, -1, 1, 2], dtype=jnp.int32)
    source = jnp.clip(owner[:, None] + offsets[direction], 0, NPART - 1).astype(jnp.int32)
    remote = source * NBL + ghost_send[source, direction, entry]
    target = jnp.where(ghost, remote, owner[:, None] * NBL + col_index).astype(jnp.int32)
    live = (jnp.arange(KMAX, dtype=jnp.int32)[None, :] < counts[:, None]).astype(jnp.float32)
    blocks = primal.reshape(R, NBT, BS)

    def one_row(row):
        picked = blocks[:, target[row]].astype(jnp.float32) * live[row][None, :, None]
        mats = op_blocks[row].astype(jnp.float32)
        return jnp.einsum('mkc,kjc->mj', picked, mats)
    applied = lax.map(one_row, rows)
    applied = jnp.transpose(applied, (1, 0, 2)).reshape(R, NSP).astype(jnp.bfloat16)
    factor = 1.0 / math.sqrt(NSP)
    reduced = jnp.dot(adjoint, applied.T, preferred_element_type=jnp.float32) * factor
    gram = jnp.dot(adjoint, primal.T, preferred_element_type=jnp.float32) * factor
    return (primal, applied, reduced, gram)
```

```python
import math

import jax
import jax.numpy as jnp
from jax import lax
from jax.sharding import PartitionSpec as P

F32 = jnp.float32
BF16 = jnp.bfloat16


def exchange(tiles, axis, groups=None):
    return lax.all_to_all(tiles, axis, 0, 0, tiled=True, axis_index_groups=groups)


def passed_along(value, axis, steps):
    count = lax.axis_size(axis)
    first, last = (max(0, -steps), min(count, count - steps))
    return lax.ppermute(value, axis, [(source, source + steps) for source in range(first, last)])


def space_groups(count):
    far, half = count // 8, count // 2
    near_of = [[h * half + f * 4 + low for h in range(2) for low in range(4)] for f in range(far)]
    far_of = [[h * half + f * 4 + low for f in range(far)] for h in range(2) for low in range(4)]
    return near_of, far_of


def total_over_space(terms):
    near, far = space_groups(lax.axis_size("space"))
    rows, cols = terms.shape
    mine = exchange(terms.reshape(8, rows // 8, cols), "space", near).sum(axis=0)
    every = exchange(jnp.broadcast_to(mine[None], (len(far[0]), *mine.shape)), "space", far)
    mine = every.sum(axis=0)
    return exchange(jnp.broadcast_to(mine[None], (8, *mine.shape)), "space", near).reshape(rows, cols)


def per_device(
    snaps_primal, snaps_adjoint, coef_primal, coef_adjoint, op_blocks, counts, col_index, ghost_send
):
    ways = lax.axis_size("snap")
    modes = coef_primal.shape[1]
    share = modes // ways
    unknowns = snaps_primal.shape[1]
    piece = unknowns // ways
    row_count, slot_count = col_index.shape
    block_size = op_blocks.shape[2]
    list_len = ghost_send.shape[2]

    primal_part = jnp.einsum("mr,ms->rs", coef_primal, snaps_primal, preferred_element_type=F32)
    primal_tiles = exchange(primal_part.astype(BF16).reshape(ways, share, unknowns), "snap")
    adjoint_part = jnp.einsum(
        "mr,mws->wrs",
        coef_adjoint,
        snaps_adjoint.reshape(-1, ways, piece),
        preferred_element_type=F32,
    )
    adjoint_tiles = exchange(adjoint_part.astype(BF16), "snap")
    primal = primal_tiles.astype(F32).sum(axis=0).astype(BF16)

    blocks = primal.reshape(share, row_count, block_size)
    outgoing = jnp.take(blocks, ghost_send[0], axis=1)
    received = jnp.stack(
        [passed_along(outgoing[:, d], "space", step) for d, step in enumerate((2, 1, -1, -2))], axis=1
    )
    extended = jnp.concatenate([blocks, received.reshape(share, 4 * list_len, block_size)], axis=1)
    picked = jnp.take(extended, col_index, axis=1)
    live = (jnp.arange(slot_count, dtype=jnp.int32)[None, :] < counts[:, None]).astype(BF16)
    picked = picked * live[None, :, :, None]
    applied = jnp.einsum("mrkc,rkjc->mrj", picked, op_blocks, preferred_element_type=F32)
    applied = applied.astype(BF16).reshape(share, unknowns)

    both = jnp.stack([applied, primal]).reshape(2 * share, ways, piece)
    both = exchange(jnp.moveaxis(both, 1, 0), "snap")
    adjoint = adjoint_tiles.astype(F32).sum(axis=0).astype(BF16)
    products = jnp.einsum("was,bs->wab", both, adjoint, preferred_element_type=F32)
    mine = exchange(products.astype(BF16), "snap").astype(F32).sum(axis=0)
    total = total_over_space(mine) * (1.0 / math.sqrt(unknowns * lax.axis_size("space")))
    return (primal, applied, total[:share].T, total[share:].T)


def solution(mesh):
    placed = (
        P("snap", "space"),
        P("snap", "space"),
        P("snap", None),
        P("snap", None),
        P("space", None, None, None),
        P("space"),
        P("space", None),
        P("space", None, None),
    )
    return jax.shard_map(
        per_device,
        mesh=mesh,
        in_specs=placed,
        out_specs=(P("snap", "space"), P("snap", "space"), P(None, "snap"), P(None, "snap")),
        check_vma=False,
    )
```

```python
import functools
import math

import jax
import jax.numpy as jnp
from jax import lax
from jax.experimental import pallas as pl
from jax.experimental.pallas import tpu as pltpu
from jax.sharding import PartitionSpec as P

F32 = jnp.float32
BF16 = jnp.bfloat16
STEPS = (2, 1, -1, -2)
NEAR = 4
PARTS = 6
PAIR = 2


def exchange(tiles, axis, groups=None):
    return lax.all_to_all(tiles, axis, 0, 0, tiled=True, axis_index_groups=groups)


def passed_along(value, axis, steps):
    count = lax.axis_size(axis)
    first, last = (max(0, -steps), min(count, count - steps))
    return lax.ppermute(value, axis, [(source, source + steps) for source in range(first, last)])


def z_groups(space):
    half, depth = space // 2, space // NEAR
    along = [[h * half + z * 2 + c for z in range(depth)] for h in range(2) for c in range(2)]
    across = [[h * half + z * 2 + c for h in range(2) for c in range(2)] for z in range(depth)]
    return along, across


def vmem():
    return pl.BlockSpec(memory_space=pltpu.VMEM)


def smem():
    return pl.BlockSpec(memory_space=pltpu.SMEM)


def sum_kernel(send_ref, tiles_ref, primal_ref, *out_refs):
    ways = tiles_ref.shape[0]
    total = tiles_ref[0].astype(F32)
    for j in range(1, ways):
        total = total + tiles_ref[j].astype(F32)
    primal_ref[...] = total.astype(BF16)
    size = out_refs[0].shape[2]
    for d, out_ref in enumerate(out_refs):
        for t in range(out_ref.shape[0]):
            start = pl.multiple_of(send_ref[d, t] * size, size)
            out_ref[t] = primal_ref[:, pl.ds(start, size)]


def sum_and_pick(tiles, ghost_send, size):
    ways, share, unknowns = tiles.shape
    lists, length = ghost_send.shape
    return pl.pallas_call(
        sum_kernel,
        out_shape=[jax.ShapeDtypeStruct((share, unknowns), BF16)]
        + [jax.ShapeDtypeStruct((length, share, size), BF16)] * lists,
        in_specs=[smem(), vmem()],
        out_specs=[vmem()] * (1 + lists),
        compiler_params=pltpu.CompilerParams(vmem_limit_bytes=8 << 20),
    )(ghost_send, tiles)


def apply_kernel(counts_ref, cols_ref, primal_ref, *refs):
    *ghost_refs, op_hbm, applied_ref, both_ref, held, op_ref, sems = refs
    rows, slots, size, _ = op_ref.shape
    count = sems.shape[0]
    part = rows // count
    copies = []
    for i in range(count):
        cut = pl.ds(i * part, part)
        copies.append(pltpu.make_async_copy(op_hbm.at[cut], op_ref.at[cut], sems.at[i]))
        copies[-1].start()
    share = primal_ref.shape[0]
    ways, _, piece = both_ref.shape
    for b in range(rows):
        held[b] = primal_ref[:, b * size : (b + 1) * size]
    at = rows
    for ghost_ref in ghost_refs:
        length = ghost_ref.shape[0]
        held[at : at + length] = ghost_ref[...]
        at += length
    per = piece // size
    for r in range(rows):
        if r % part == 0:
            copies[r // part].wait()
        total = None
        for k in range(slots):
            block = held[cols_ref[r, k]]
            block = jnp.where(k < counts_ref[r], block, jnp.zeros_like(block))
            term = lax.dot_general(
                block, op_ref[r, k], (((1,), (1,)), ((), ())), preferred_element_type=F32
            )
            total = term if total is None else total + term
        out = total.astype(BF16)
        applied_ref[:, r * size : (r + 1) * size] = out
        both_ref[r // per, :share, (r % per) * size : (r % per + 1) * size] = out
    for w in range(ways):
        both_ref[w, share:, :] = primal_ref[:, w * piece : (w + 1) * piece]


def applied_and_laid_out(counts, cols, primal, ghosts, op_blocks, ways):
    share, unknowns = primal.shape
    rows, slots, size, _ = op_blocks.shape
    held = rows + sum(g.shape[0] for g in ghosts)
    return pl.pallas_call(
        apply_kernel,
        out_shape=[
            jax.ShapeDtypeStruct((share, unknowns), BF16),
            jax.ShapeDtypeStruct((ways, 2 * share, unknowns // ways), BF16),
        ],
        in_specs=[smem(), smem()]
        + [vmem()] * (1 + len(ghosts))
        + [pl.BlockSpec(memory_space=pltpu.HBM)],
        out_specs=[vmem(), vmem()],
        scratch_shapes=[
            pltpu.VMEM((held, share, size), BF16),
            pltpu.VMEM(op_blocks.shape, BF16),
            pltpu.SemaphoreType.DMA((PARTS,)),
        ],
        compiler_params=pltpu.CompilerParams(vmem_limit_bytes=60 << 20),
    )(counts, cols, primal, *ghosts, op_blocks)


def per_device(
    snaps_primal, snaps_adjoint, coef_primal, coef_adjoint, op_blocks, counts, col_index, ghost_send
):
    ways, space = lax.axis_size("snap"), lax.axis_size("space")
    runs = ways // PAIR
    modes = coef_primal.shape[1]
    share = modes // ways
    unknowns = snaps_primal.shape[1]
    piece = unknowns // ways
    size = op_blocks.shape[2]
    along_z, across_z = z_groups(space)
    flat_groups = [[p * ways + s for s in range(ways) for p in group] for group in across_z]
    along_x = [[x * PAIR + y for x in range(runs)] for y in range(PAIR)]

    primal_part = jnp.einsum("mr,ms->rs", coef_primal, snaps_primal, preferred_element_type=F32)
    primal_tiles = exchange(primal_part.astype(BF16).reshape(ways, share, unknowns), "snap")

    adjoint_part = jnp.einsum("mr,ms->rs", coef_adjoint, snaps_adjoint, preferred_element_type=F32)
    adjoint_tiles = jnp.moveaxis(adjoint_part.astype(BF16).reshape(modes, runs, PAIR * piece), 1, 0)
    primal, *outgoing = sum_and_pick(primal_tiles, ghost_send[0], size)
    adjoint_tiles, primal = lax.optimization_barrier((adjoint_tiles, primal))
    adjoint_tiles = exchange(adjoint_tiles, "snap", along_x)
    adjoint_run = adjoint_tiles.astype(F32).sum(axis=0)
    y = lax.axis_index("snap") % PAIR
    own = lax.dynamic_slice_in_dim(adjoint_run, y * piece, piece, axis=1)
    other = lax.dynamic_slice_in_dim(adjoint_run, (1 - y) * piece, piece, axis=1).astype(BF16)
    arrived = lax.ppermute(other, "snap", [(s, s ^ 1) for s in range(ways)])
    adjoint = (own + arrived.astype(F32)).astype(BF16)

    ghosts = [passed_along(o, "space", step) for o, step in zip(outgoing, STEPS)]
    applied, both = applied_and_laid_out(counts, col_index, primal, ghosts, op_blocks, ways)

    both = exchange(both, "snap")
    products = jnp.einsum("was,bs->wab", both, adjoint, preferred_element_type=F32).astype(BF16)
    rows = 2 * share // NEAR
    tiles = exchange(products.reshape(ways * NEAR, rows, modes), ("space", "snap"), flat_groups)
    mine = tiles.astype(F32).sum(axis=0).astype(BF16)
    every = exchange(jnp.broadcast_to(mine[None], (space // NEAR, rows, modes)), "space", along_z)
    factor = 1.0 / math.sqrt(unknowns * space)
    mine = every.astype(F32).sum(axis=0) * factor
    total = exchange(jnp.broadcast_to(mine[None], (NEAR, rows, modes)), "space", across_z)
    total = total.reshape(2 * share, modes)
    return (primal, applied, total[:share].T, total[share:].T)


def solution(mesh):
    placed = (
        P("snap", "space"),
        P("snap", "space"),
        P("snap", None),
        P("snap", None),
        P("space", None, None, None),
        P("space"),
        P("space", None),
        P("space", None, None),
    )
    return jax.shard_map(
        per_device,
        mesh=mesh,
        in_specs=placed,
        out_specs=(P("snap", "space"), P("snap", "space"), P(None, "snap"), P(None, "snap")),
        check_vma=False,
    )
```

```python
import math

import jax
import jax.numpy as jnp
from jax import lax
from jax.experimental import pallas as pl
from jax.experimental.pallas import tpu as pltpu
from jax.sharding import PartitionSpec as P

F32 = jnp.float32
BF16 = jnp.bfloat16
NEAR = 4
PAIR = 2
PARTS = 6
SMALL, LARGE = 12 << 20, 58 << 20


def exchange(tiles, axis, groups=None):
    return lax.all_to_all(tiles, axis, 0, 0, tiled=True, axis_index_groups=groups)


def swapped(value, axis, pairs):
    return lax.ppermute(value, axis, [(a, b) for a, b in pairs] + [(b, a) for a, b in pairs])


def space_pairings(count):
    far_odd = [(p, p + 2) for p in range(count - 2) if p % 4 >= 2]
    far_even = [(p, p + 2) for p in range(count - 2) if p % 4 < 2]
    near_odd = [(p, p + 1) for p in range(1, count - 1, 2)]
    near_even = [(p, p + 1) for p in range(0, count - 1, 2)]
    return far_odd, near_odd, far_even, near_even


def lists_of_pairings(place):
    far, near = lax.rem(place, 4) >= 2, lax.rem(place, 2) == 1
    for up, below, above in ((far, 0, 3), (near, 1, 2), (~far, 0, 3), (~near, 1, 2)):
        yield jnp.where(up, below, above), jnp.where(up, above, below)


def vmem():
    return pl.BlockSpec(memory_space=pltpu.VMEM)


def smem():
    return pl.BlockSpec(memory_space=pltpu.SMEM)


def limit(size):
    return pltpu.CompilerParams(vmem_limit_bytes=size)


def split_kernel(side_ref, tiles_ref, own_ref, other_ref):
    share = own_ref.shape[0]

    def summed(start):
        rows = pl.ds(pl.multiple_of(start, share), share)
        total = tiles_ref[0, rows].astype(F32)
        for j in range(1, tiles_ref.shape[0]):
            total = total + tiles_ref[j, rows].astype(F32)
        return total

    other_ref[...] = summed((1 - side_ref[0]) * share).astype(BF16)
    own_ref[...] = summed(side_ref[0] * share)


def summed_halves(side, tiles):
    _, rows, unknowns = tiles.shape
    share = rows // PAIR
    return pl.pallas_call(
        split_kernel,
        out_shape=[
            jax.ShapeDtypeStruct((share, unknowns), F32),
            jax.ShapeDtypeStruct((share, unknowns), BF16),
        ],
        in_specs=[smem(), vmem()],
        out_specs=[vmem(), vmem()],
        compiler_params=limit(SMALL),
    )(side, tiles)


def pick_kernel(place_ref, send_ref, own_ref, arrived_ref, primal_ref, *out_refs):
    primal_ref[...] = (own_ref[...] + arrived_ref[...].astype(F32)).astype(BF16)
    size = out_refs[0].shape[2]
    for (sent, _), out_ref in zip(lists_of_pairings(place_ref[0]), out_refs):
        for t in range(out_ref.shape[0]):
            start = pl.multiple_of(send_ref[sent, t] * size, size)
            out_ref[t] = primal_ref[:, pl.ds(start, size)]


def sum_and_pick(place, lists, own, arrived, size):
    share, unknowns = own.shape
    count, length = lists.shape
    return pl.pallas_call(
        pick_kernel,
        out_shape=[jax.ShapeDtypeStruct((share, unknowns), BF16)]
        + [jax.ShapeDtypeStruct((length, share, size), BF16)] * count,
        in_specs=[smem(), smem(), vmem(), vmem()],
        out_specs=[vmem()] * (1 + count),
        compiler_params=limit(SMALL),
    )(place, lists, own, arrived)


def bring_kernel(_, op_hbm, op_ref, sems):
    part = op_hbm.shape[0] // PARTS
    copies = []
    for i in range(PARTS):
        cut = pl.ds(i * part, part)
        copies.append(pltpu.make_async_copy(op_hbm.at[cut], op_ref.at[cut], sems.at[i]))
        copies[-1].start()
    for copy in copies:
        copy.wait()


def brought_in(after, op_blocks):
    hbm = pl.BlockSpec(memory_space=pltpu.HBM)
    return pl.pallas_call(
        bring_kernel,
        out_shape=pltpu.VMEM(op_blocks.shape, BF16),
        in_specs=[hbm, hbm],
        out_specs=vmem(),
        scratch_shapes=[pltpu.SemaphoreType.DMA((PARTS,))],
        compiler_params=limit(LARGE),
    )(after, op_blocks)


def apply_kernel(place_ref, side_ref, counts_ref, cols_ref, primal_ref, *refs):
    *ghost_refs, op_ref, applied_ref, mine_ref, other_ref, held, halves = refs
    rows, slots, size, _ = op_ref.shape
    share = primal_ref.shape[0]
    half = mine_ref.shape[1]
    per = half // size
    for b in range(rows):
        held[b] = primal_ref[:, b * size : (b + 1) * size]
    for (_, received), ghost_ref in zip(lists_of_pairings(place_ref[0]), ghost_refs):
        length = ghost_ref.shape[0]
        held[pl.ds(rows + received * length, length)] = ghost_ref[...]
    for r in range(rows):
        blocks = []
        for k in range(slots):
            block = held[cols_ref[r, k]]
            blocks.append(jnp.where(k < counts_ref[r], block, jnp.zeros_like(block)))
        out = lax.dot_general(
            jnp.concatenate(blocks, axis=1),
            jnp.concatenate([op_ref[r, k] for k in range(slots)], axis=1),
            (((1,), (1,)), ((), ())),
            preferred_element_type=F32,
        ).astype(BF16)
        applied_ref[:, r * size : (r + 1) * size] = out
        halves[r // per, :, (r % per) * size : (r % per + 1) * size] = out
    for ref, h in ((other_ref, 1 - side_ref[0]), (mine_ref, side_ref[0])):
        ref[:share] = halves[h]
        ref[share:] = primal_ref[:, pl.ds(pl.multiple_of(h * half, half), half)]


def applied_and_halves(place, side, counts, cols, primal, ghosts, op_blocks):
    share, unknowns = primal.shape
    rows, slots, size, _ = op_blocks.shape
    held = rows + sum(g.shape[0] for g in ghosts)
    half = jax.ShapeDtypeStruct((2 * share, unknowns // PAIR), BF16)
    return pl.pallas_call(
        apply_kernel,
        out_shape=[jax.ShapeDtypeStruct((share, unknowns), BF16), half, half],
        in_specs=[smem()] * 4 + [vmem()] * (2 + len(ghosts)),
        out_specs=[vmem()] * 3,
        scratch_shapes=[
            pltpu.VMEM((held, share, size), BF16),
            pltpu.VMEM((PAIR, share, unknowns // PAIR), BF16),
        ],
        compiler_params=limit(SMALL),
    )(place, side, counts, cols, primal, *ghosts, op_blocks)


def per_device(
    snaps_primal, snaps_adjoint, coef_primal, coef_adjoint, op_blocks, counts, col_index, ghost_send
):
    ways, space = lax.axis_size("snap"), lax.axis_size("space")
    runs = ways // PAIR
    modes = coef_primal.shape[1]
    share = modes // ways
    unknowns = snaps_primal.shape[1]
    half = unknowns // PAIR
    size = op_blocks.shape[2]
    side = lax.axis_index("snap") % PAIR
    along_x = [[x * PAIR + y for x in range(runs)] for y in range(PAIR)]
    pair = [(x * PAIR, x * PAIR + 1) for x in range(runs)]
    deep = space // 2
    along_z = [[h * deep + z * 2 + c for z in range(deep // 2)] for h in range(2) for c in range(2)]
    across_z = [[h * deep + z * 2 + c for h in range(2) for c in range(2)] for z in range(deep // 2)]
    around = [
        [p * ways + x * PAIR + y for y in range(PAIR) for p in group]
        for group in across_z
        for x in range(runs)
    ]
    sides = side.reshape(1).astype(jnp.int32)
    place = lax.axis_index("space").reshape(1).astype(jnp.int32)

    primal_part = jnp.einsum("mr,ms->rs", coef_primal, snaps_primal, preferred_element_type=F32)
    primal_part, snaps_adjoint = lax.optimization_barrier((primal_part.astype(BF16), snaps_adjoint))
    primal_tiles = primal_part.reshape(runs, PAIR * share, unknowns)
    primal_tiles = exchange(primal_tiles, "snap", along_x)

    adjoint_part = jnp.einsum("mr,ms->rs", coef_adjoint, snaps_adjoint, preferred_element_type=F32)
    adjoint_part = adjoint_part.astype(BF16)
    adjoint_own = lax.dynamic_slice_in_dim(adjoint_part, side * half, half, axis=1)
    adjoint_other = lax.dynamic_slice_in_dim(adjoint_part, (1 - side) * half, half, axis=1)
    adjoint_other = swapped(adjoint_other, "snap", pair)

    own, other = summed_halves(sides, primal_tiles)
    adjoint = (adjoint_own.astype(F32) + adjoint_other.astype(F32)).astype(BF16)
    _, adjoint = lax.optimization_barrier((other, adjoint))
    arrived = swapped(other, "snap", pair)
    adjoint = exchange(adjoint.reshape(runs, modes // runs, half), "snap", along_x)
    adjoint = adjoint.astype(F32).sum(axis=0).astype(BF16)

    primal, *outgoing = sum_and_pick(place, ghost_send[0], own, arrived, size)
    ghosts = [swapped(o, "space", w) for o, w in zip(outgoing, space_pairings(space))]
    op_near = brought_in(outgoing[-1], op_blocks)
    *ghosts, adjoint = lax.optimization_barrier((*ghosts, adjoint))
    adjoint = exchange(jnp.broadcast_to(adjoint[None], (runs, *adjoint.shape)), "snap", along_x)
    adjoint = adjoint.reshape(modes, half)
    applied, mine, other = applied_and_halves(place, sides, counts, col_index, primal, ghosts, op_near)
    arrived = swapped(other, "snap", pair)

    def product(rows):
        return jnp.einsum("as,bs->ab", rows, adjoint, preferred_element_type=F32).astype(BF16)

    here, there = product(mine), product(arrived)
    first = side == 0
    products = jnp.stack([jnp.where(first, here, there), jnp.where(first, there, here)])
    rows = 2 * share // NEAR
    tiles = exchange(products.reshape(PAIR * NEAR, rows, modes), ("space", "snap"), around)
    total = tiles.astype(F32).sum(axis=0).astype(BF16)
    every = exchange(jnp.broadcast_to(total[None], (deep // 2, rows, modes)), "space", along_z)
    total = every.astype(F32).sum(axis=0) * (1.0 / math.sqrt(unknowns * space))
    total = exchange(jnp.broadcast_to(total[None], (NEAR, rows, modes)), "space", across_z)
    total = total.reshape(2 * share, modes)
    return (primal, applied, total[:share].T, total[share:].T)


def solution(mesh):
    placed = (
        P("snap", "space"),
        P("snap", "space"),
        P("snap", None),
        P("snap", None),
        P("space", None, None, None),
        P("space"),
        P("space", None),
        P("space", None, None),
    )
    return jax.shard_map(
        per_device,
        mesh=mesh,
        in_specs=placed,
        out_specs=(P("snap", "space"), P("snap", "space"), P(None, "snap"), P(None, "snap")),
        check_vma=False,
    )
```

```python
import math

import jax
import jax.numpy as jnp
from jax import lax
from jax.experimental import pallas as pl
from jax.experimental.pallas import tpu as pltpu
from jax.sharding import PartitionSpec as P

F32 = jnp.float32
BF16 = jnp.bfloat16
NEAR = 4
PARTS = 6
SMALL, LARGE = 12 << 20, 58 << 20


def exchange(tiles, axis, groups=None):
    return lax.all_to_all(tiles, axis, 0, 0, tiled=True, axis_index_groups=groups)


def swapped(value, axis, pairs):
    return lax.ppermute(value, axis, [(a, b) for a, b in pairs] + [(b, a) for a, b in pairs])


def space_pairings(count):
    far_odd = [(p, p + 2) for p in range(count - 2) if p % 4 >= 2]
    far_even = [(p, p + 2) for p in range(count - 2) if p % 4 < 2]
    near_odd = [(p, p + 1) for p in range(1, count - 1, 2)]
    near_even = [(p, p + 1) for p in range(0, count - 1, 2)]
    return far_odd, near_odd, far_even, near_even


def lists_of_pairings(place):
    far, near = lax.rem(place, 4) >= 2, lax.rem(place, 2) == 1
    for up, below, above in ((far, 0, 3), (near, 1, 2), (~far, 0, 3), (~near, 1, 2)):
        yield jnp.where(up, below, above), jnp.where(up, above, below)


def vmem():
    return pl.BlockSpec(memory_space=pltpu.VMEM)


def smem():
    return pl.BlockSpec(memory_space=pltpu.SMEM)


def limit(size):
    return pltpu.CompilerParams(vmem_limit_bytes=size)


def pick_kernel(place_ref, send_ref, tiles_ref, primal_ref, *out_refs):
    total = tiles_ref[0].astype(F32)
    for j in range(1, tiles_ref.shape[0]):
        total = total + tiles_ref[j].astype(F32)
    primal_ref[...] = total.astype(BF16)
    size = out_refs[0].shape[2]
    for (sent, _), out_ref in zip(lists_of_pairings(place_ref[0]), out_refs):
        for t in range(out_ref.shape[0]):
            start = pl.multiple_of(send_ref[sent, t] * size, size)
            out_ref[t] = primal_ref[:, pl.ds(start, size)]


def sum_and_pick(place, lists, tiles, size):
    _, share, unknowns = tiles.shape
    count, length = lists.shape
    return pl.pallas_call(
        pick_kernel,
        out_shape=[jax.ShapeDtypeStruct((share, unknowns), BF16)]
        + [jax.ShapeDtypeStruct((length, share, size), BF16)] * count,
        in_specs=[smem(), smem(), vmem()],
        out_specs=[vmem()] * (1 + count),
        compiler_params=limit(SMALL),
    )(place, lists, tiles)


def apply_kernel(place_ref, counts_ref, cols_ref, primal_ref, *refs):
    *ghost_refs, op_hbm, applied_ref, both_ref, held, op_ref, sems = refs
    rows, slots, size, _ = op_ref.shape
    share = primal_ref.shape[0]
    ways, _, piece = both_ref.shape
    per = piece // size
    part = rows // PARTS
    copies = []
    for i in range(PARTS):
        cut = pl.ds(i * part, part)
        copies.append(pltpu.make_async_copy(op_hbm.at[cut], op_ref.at[cut], sems.at[i]))
        copies[-1].start()
    for b in range(rows):
        held[b] = primal_ref[:, b * size : (b + 1) * size]
    for (_, received), ghost_ref in zip(lists_of_pairings(place_ref[0]), ghost_refs):
        length = ghost_ref.shape[0]
        held[pl.ds(rows + received * length, length)] = ghost_ref[...]
    for w in range(ways):
        both_ref[w, share:, :] = primal_ref[:, w * piece : (w + 1) * piece]
    for r in range(rows):
        if r % part == 0:
            copies[r // part].wait()
        blocks = []
        for k in range(slots):
            block = held[cols_ref[r, k]]
            blocks.append(jnp.where(k < counts_ref[r], block, jnp.zeros_like(block)))
        out = lax.dot_general(
            jnp.concatenate(blocks, axis=1),
            jnp.concatenate([op_ref[r, k] for k in range(slots)], axis=1),
            (((1,), (1,)), ((), ())),
            preferred_element_type=F32,
        ).astype(BF16)
        applied_ref[:, r * size : (r + 1) * size] = out
        both_ref[r // per, :share, (r % per) * size : (r % per + 1) * size] = out


def applied_and_laid_out(place, counts, cols, primal, ghosts, op_blocks, ways):
    share, unknowns = primal.shape
    rows, slots, size, _ = op_blocks.shape
    held = rows + sum(g.shape[0] for g in ghosts)
    return pl.pallas_call(
        apply_kernel,
        out_shape=[
            jax.ShapeDtypeStruct((share, unknowns), BF16),
            jax.ShapeDtypeStruct((ways, 2 * share, unknowns // ways), BF16),
        ],
        in_specs=[smem()] * 3
        + [vmem()] * (1 + len(ghosts))
        + [pl.BlockSpec(memory_space=pltpu.HBM)],
        out_specs=[vmem(), vmem()],
        scratch_shapes=[
            pltpu.VMEM((held, share, size), BF16),
            pltpu.VMEM(op_blocks.shape, BF16),
            pltpu.SemaphoreType.DMA((PARTS,)),
        ],
        compiler_params=limit(LARGE),
    )(place, counts, cols, primal, *ghosts, op_blocks)


def per_device(
    snaps_primal, snaps_adjoint, coef_primal, coef_adjoint, op_blocks, counts, col_index, ghost_send
):
    ways, space = lax.axis_size("snap"), lax.axis_size("space")
    modes = coef_primal.shape[1]
    share = modes // ways
    unknowns = snaps_primal.shape[1]
    piece = unknowns // ways
    size = op_blocks.shape[2]
    deep = space // 2
    along_z = [[h * deep + z * 2 + c for z in range(deep // 2)] for h in range(2) for c in range(2)]
    across_z = [[h * deep + z * 2 + c for h in range(2) for c in range(2)] for z in range(deep // 2)]
    around = [[p * ways + s for s in range(ways) for p in group] for group in across_z]
    place = lax.axis_index("space").reshape(1).astype(jnp.int32)

    primal_part = jnp.einsum("mr,ms->rs", coef_primal, snaps_primal, preferred_element_type=F32)
    primal_tiles = exchange(primal_part.astype(BF16).reshape(ways, share, unknowns), "snap")

    adjoint_part = jnp.einsum("mr,ms->rs", coef_adjoint, snaps_adjoint, preferred_element_type=F32)
    adjoint_tiles = jnp.moveaxis(adjoint_part.astype(BF16).reshape(modes, ways, piece), 1, 0)

    primal, *outgoing = sum_and_pick(place, ghost_send[0], primal_tiles, size)
    adjoint_tiles, _ = lax.optimization_barrier((adjoint_tiles, primal))
    adjoint_tiles = exchange(adjoint_tiles, "snap")
    ghosts = [swapped(o, "space", w) for o, w in zip(outgoing, space_pairings(space))]
    applied, both = applied_and_laid_out(place, counts, col_index, primal, ghosts, op_blocks, ways)

    both = exchange(both, "snap")
    adjoint = adjoint_tiles.astype(F32).sum(axis=0).astype(BF16)
    products = jnp.einsum("was,bs->wab", both, adjoint, preferred_element_type=F32).astype(BF16)
    rows = 2 * share // NEAR
    tiles = exchange(products.reshape(ways * NEAR, rows, modes), ("space", "snap"), around)
    total = tiles.astype(F32).sum(axis=0).astype(BF16)
    every = exchange(jnp.broadcast_to(total[None], (deep // 2, rows, modes)), "space", along_z)
    total = every.astype(F32).sum(axis=0) * (1.0 / math.sqrt(unknowns * space))
    total = exchange(jnp.broadcast_to(total[None], (NEAR, rows, modes)), "space", across_z)
    total = total.reshape(2 * share, modes)
    return (primal, applied, total[:share].T, total[share:].T)


def solution(mesh):
    placed = (
        P("snap", "space"),
        P("snap", "space"),
        P("snap", None),
        P("snap", None),
        P("space", None, None, None),
        P("space"),
        P("space", None),
        P("space", None, None),
    )
    return jax.shard_map(
        per_device,
        mesh=mesh,
        in_specs=placed,
        out_specs=(P("snap", "space"), P("snap", "space"), P(None, "snap"), P(None, "snap")),
        check_vma=False,
    )
```

```python
import math

import jax
import jax.numpy as jnp
from jax import lax
from jax.experimental import pallas as pl
from jax.experimental.pallas import tpu as pltpu
from jax.sharding import PartitionSpec as P

F32 = jnp.float32
BF16 = jnp.bfloat16
NEAR = 4
PARTS = 6
SMALL, LARGE = 12 << 20, 58 << 20


def exchange(tiles, axis, groups=None):
    return lax.all_to_all(tiles, axis, 0, 0, tiled=True, axis_index_groups=groups)


def swapped(value, axis, pairs):
    return lax.ppermute(value, axis, [(a, b) for a, b in pairs] + [(b, a) for a, b in pairs])


def space_pairings(count):
    far_odd = [(p, p + 2) for p in range(count - 2) if p % 4 >= 2]
    far_even = [(p, p + 2) for p in range(count - 2) if p % 4 < 2]
    near_odd = [(p, p + 1) for p in range(1, count - 1, 2)]
    near_even = [(p, p + 1) for p in range(0, count - 1, 2)]
    return far_odd, near_odd, far_even, near_even


def lists_of_pairings(place):
    far, near = lax.rem(place, 4) >= 2, lax.rem(place, 2) == 1
    for up, below, above in ((far, 0, 3), (near, 1, 2), (~far, 0, 3), (~near, 1, 2)):
        yield jnp.where(up, below, above), jnp.where(up, above, below)


def vmem():
    return pl.BlockSpec(memory_space=pltpu.VMEM)


def smem():
    return pl.BlockSpec(memory_space=pltpu.SMEM)


def limit(size):
    return pltpu.CompilerParams(vmem_limit_bytes=size)


def pick_kernel(place_ref, send_ref, tiles_ref, primal_ref, *out_refs):
    total = tiles_ref[0].astype(F32)
    for j in range(1, tiles_ref.shape[0]):
        total = total + tiles_ref[j].astype(F32)
    primal_ref[...] = total.astype(BF16)
    size = out_refs[0].shape[2]
    for (sent, _), out_ref in zip(lists_of_pairings(place_ref[0]), out_refs):
        for t in range(out_ref.shape[0]):
            start = pl.multiple_of(send_ref[sent, t] * size, size)
            out_ref[t] = primal_ref[:, pl.ds(start, size)]


def sum_and_pick(place, lists, tiles, size):
    _, share, unknowns = tiles.shape
    count, length = lists.shape
    return pl.pallas_call(
        pick_kernel,
        out_shape=[jax.ShapeDtypeStruct((share, unknowns), BF16)]
        + [jax.ShapeDtypeStruct((length, share, size), BF16)] * count,
        in_specs=[smem(), smem(), vmem()],
        out_specs=[vmem()] * (1 + count),
        compiler_params=limit(SMALL),
    )(place, lists, tiles)


def apply_kernel(place_ref, counts_ref, cols_ref, primal_ref, *refs):
    *ghost_refs, op_hbm, applied_ref, both_ref, held, op_ref, sems = refs
    rows, slots, size, _ = op_ref.shape
    share = primal_ref.shape[0]
    ways, _, piece = both_ref.shape
    per = piece // size
    part = rows // PARTS
    copies = []
    for i in range(PARTS):
        cut = pl.ds(i * part, part)
        copies.append(pltpu.make_async_copy(op_hbm.at[cut], op_ref.at[cut], sems.at[i]))
        copies[-1].start()
    for b in range(rows):
        held[b] = primal_ref[:, b * size : (b + 1) * size]
    for (_, received), ghost_ref in zip(lists_of_pairings(place_ref[0]), ghost_refs):
        length = ghost_ref.shape[0]
        held[pl.ds(rows + received * length, length)] = ghost_ref[...]
    for w in range(ways):
        both_ref[w, share:, :] = primal_ref[:, w * piece : (w + 1) * piece]
    for r in range(rows):
        if r % part == 0:
            copies[r // part].wait()
        blocks = []
        for k in range(slots):
            block = held[cols_ref[k, r]]
            blocks.append(jnp.where(k < counts_ref[r], block, jnp.zeros_like(block)))
        out = lax.dot_general(
            jnp.concatenate(blocks, axis=1),
            jnp.concatenate([op_ref[r, k] for k in range(slots)], axis=1),
            (((1,), (1,)), ((), ())),
            preferred_element_type=F32,
        ).astype(BF16)
        applied_ref[:, r * size : (r + 1) * size] = out
        both_ref[r // per, :share, (r % per) * size : (r % per + 1) * size] = out


def applied_and_laid_out(place, counts, cols, primal, ghosts, op_blocks, ways):
    share, unknowns = primal.shape
    rows, slots, size, _ = op_blocks.shape
    held = rows + sum(g.shape[0] for g in ghosts)
    return pl.pallas_call(
        apply_kernel,
        out_shape=[
            jax.ShapeDtypeStruct((share, unknowns), BF16),
            jax.ShapeDtypeStruct((ways, 2 * share, unknowns // ways), BF16),
        ],
        in_specs=[smem()] * 3
        + [vmem()] * (1 + len(ghosts))
        + [pl.BlockSpec(memory_space=pltpu.HBM)],
        out_specs=[vmem(), vmem()],
        scratch_shapes=[
            pltpu.VMEM((held, share, size), BF16),
            pltpu.VMEM(op_blocks.shape, BF16),
            pltpu.SemaphoreType.DMA((PARTS,)),
        ],
        compiler_params=limit(LARGE),
    )(place, counts, cols, primal, *ghosts, op_blocks)


def per_device(
    snaps_primal, snaps_adjoint, coef_primal, coef_adjoint, op_blocks, counts, col_index, ghost_send
):
    ways, space = lax.axis_size("snap"), lax.axis_size("space")
    modes = coef_primal.shape[1]
    share = modes // ways
    unknowns = snaps_primal.shape[1]
    piece = unknowns // ways
    size = op_blocks.shape[2]
    deep = space // 2
    along_z = [[h * deep + z * 2 + c for z in range(deep // 2)] for h in range(2) for c in range(2)]
    across_z = [[h * deep + z * 2 + c for h in range(2) for c in range(2)] for z in range(deep // 2)]
    turns = [0, 3, 4, 7, 2, 1, 6, 5]
    around = [[p * ways + s for s in turns for p in group] for group in across_z]
    place = lax.axis_index("space").reshape(1).astype(jnp.int32)

    coef_turned = jnp.concatenate([coef_primal[:, s * share : (s + 1) * share] for s in turns], axis=1)
    primal_part = jnp.einsum("mr,ms->rs", coef_turned, snaps_primal, preferred_element_type=F32)
    primal_tiles = primal_part.astype(BF16).reshape(ways, share, unknowns)
    primal_tiles = exchange(primal_tiles, "snap", [turns])

    adjoint_part = jnp.einsum("mr,ms->rs", coef_adjoint, snaps_adjoint, preferred_element_type=F32)
    adjoint_tiles = jnp.moveaxis(adjoint_part.astype(BF16).reshape(modes, ways, piece), 1, 0)

    primal, *outgoing = sum_and_pick(place, ghost_send[0], primal_tiles, size)
    adjoint_tiles, _ = lax.optimization_barrier((adjoint_tiles, primal))
    adjoint_tiles = exchange(adjoint_tiles, "snap", [turns])
    ghosts = [swapped(o, "space", w) for o, w in zip(outgoing, space_pairings(space))]
    applied, both = applied_and_laid_out(place, counts, col_index.T, primal, ghosts, op_blocks, ways)

    both = exchange(both, "snap", [turns])
    adjoint = adjoint_tiles.astype(F32).sum(axis=0).astype(BF16)
    products = jnp.einsum("was,bs->wab", both, adjoint, preferred_element_type=F32).astype(BF16)
    rows = 2 * share // NEAR
    tiles = exchange(products.reshape(ways * NEAR, rows, modes), ("space", "snap"), around)
    total = tiles.astype(F32).sum(axis=0).astype(BF16)
    every = exchange(jnp.broadcast_to(total[None], (deep // 2, rows, modes)), "space", along_z)
    total = every.astype(F32).sum(axis=0) * (1.0 / math.sqrt(unknowns * space))
    total = exchange(jnp.broadcast_to(total[None], (NEAR, rows, modes)), "space", across_z)
    total = total.reshape(2 * share, modes)
    return (primal, applied, total[:share].T, total[share:].T)


def solution(mesh):
    placed = (
        P("snap", "space"),
        P("snap", "space"),
        P("snap", None),
        P("snap", None),
        P("space", None, None, None),
        P("space"),
        P("space", None),
        P("space", None, None),
    )
    return jax.shard_map(
        per_device,
        mesh=mesh,
        in_specs=placed,
        out_specs=(P("snap", "space"), P("snap", "space"), P(None, "snap"), P(None, "snap")),
        check_vma=False,
    )
```

```python
import math

import jax
import jax.numpy as jnp
from jax import lax
from jax.experimental import pallas as pl
from jax.experimental.pallas import tpu as pltpu
from jax.sharding import PartitionSpec as P

F32 = jnp.float32
BF16 = jnp.bfloat16
NEAR = 4
PARTS = 6
SMALL, LARGE = 12 << 20, 58 << 20


def exchange(tiles, axis, groups=None):
    return lax.all_to_all(tiles, axis, 0, 0, tiled=True, axis_index_groups=groups)


def swapped(value, axis, pairs):
    return lax.ppermute(value, axis, [(a, b) for a, b in pairs] + [(b, a) for a, b in pairs])


def space_pairings(count):
    far_odd = [(p, p + 2) for p in range(count - 2) if p % 4 >= 2]
    far_even = [(p, p + 2) for p in range(count - 2) if p % 4 < 2]
    near_odd = [(p, p + 1) for p in range(1, count - 1, 2)]
    near_even = [(p, p + 1) for p in range(0, count - 1, 2)]
    return far_odd, near_odd, far_even, near_even


def lists_of_pairings(place):
    far, near = lax.rem(place, 4) >= 2, lax.rem(place, 2) == 1
    for up, below, above in ((far, 0, 3), (near, 1, 2), (~far, 0, 3), (~near, 1, 2)):
        yield jnp.where(up, below, above), jnp.where(up, above, below)


def vmem():
    return pl.BlockSpec(memory_space=pltpu.VMEM)


def smem():
    return pl.BlockSpec(memory_space=pltpu.SMEM)


def limit(size):
    return pltpu.CompilerParams(vmem_limit_bytes=size)


def pick_kernel(place_ref, send_ref, tiles_ref, primal_ref, *out_refs):
    total = tiles_ref[0].astype(F32)
    for j in range(1, tiles_ref.shape[0]):
        total = total + tiles_ref[j].astype(F32)
    primal_ref[...] = total.astype(BF16)
    size = out_refs[0].shape[2]
    for (sent, _), out_ref in zip(lists_of_pairings(place_ref[0]), out_refs):
        for t in range(out_ref.shape[0]):
            start = pl.multiple_of(send_ref[sent, t] * size, size)
            out_ref[t] = primal_ref[:, pl.ds(start, size)]


def sum_and_pick(place, lists, tiles, size):
    _, share, unknowns = tiles.shape
    count, length = lists.shape
    return pl.pallas_call(
        pick_kernel,
        out_shape=[jax.ShapeDtypeStruct((share, unknowns), BF16)]
        + [jax.ShapeDtypeStruct((length, share, size), BF16)] * count,
        in_specs=[smem(), smem(), vmem()],
        out_specs=[vmem()] * (1 + count),
        compiler_params=limit(SMALL),
    )(place, lists, tiles)


def apply_kernel(place_ref, counts_ref, cols_ref, primal_ref, *refs):
    *ghost_refs, op_hbm, applied_ref, both_ref, held, op_ref, sems = refs
    rows, slots, size, _ = op_ref.shape
    share = primal_ref.shape[0]
    ways, _, piece = both_ref.shape
    per = piece // size
    part = rows // PARTS
    copies = []
    for i in range(PARTS):
        cut = pl.ds(i * part, part)
        copies.append(pltpu.make_async_copy(op_hbm.at[cut], op_ref.at[cut], sems.at[i]))
        copies[-1].start()
    for b in range(rows):
        held[b] = primal_ref[:, b * size : (b + 1) * size]
    for (_, received), ghost_ref in zip(lists_of_pairings(place_ref[0]), ghost_refs):
        length = ghost_ref.shape[0]
        held[pl.ds(rows + received * length, length)] = ghost_ref[...]
    for w in range(ways):
        both_ref[w, share:, :] = primal_ref[:, w * piece : (w + 1) * piece]
    for r in range(rows):
        if r % part == 0:
            copies[r // part].wait()
        blocks = []
        for k in range(slots):
            block = held[cols_ref[k, r]]
            blocks.append(jnp.where(k < counts_ref[r], block, jnp.zeros_like(block)))
        out = lax.dot_general(
            jnp.concatenate(blocks, axis=1),
            jnp.concatenate([op_ref[r, k] for k in range(slots)], axis=1),
            (((1,), (1,)), ((), ())),
            preferred_element_type=F32,
        ).astype(BF16)
        applied_ref[:, r * size : (r + 1) * size] = out
        both_ref[r // per, :share, (r % per) * size : (r % per + 1) * size] = out


def applied_and_laid_out(place, counts, cols, primal, ghosts, op_blocks, ways):
    share, unknowns = primal.shape
    rows, slots, size, _ = op_blocks.shape
    held = rows + sum(g.shape[0] for g in ghosts)
    return pl.pallas_call(
        apply_kernel,
        out_shape=[
            jax.ShapeDtypeStruct((share, unknowns), BF16),
            jax.ShapeDtypeStruct((ways, 2 * share, unknowns // ways), BF16),
        ],
        in_specs=[smem()] * 3
        + [vmem()] * (1 + len(ghosts))
        + [pl.BlockSpec(memory_space=pltpu.HBM)],
        out_specs=[vmem(), vmem()],
        scratch_shapes=[
            pltpu.VMEM((held, share, size), BF16),
            pltpu.VMEM(op_blocks.shape, BF16),
            pltpu.SemaphoreType.DMA((PARTS,)),
        ],
        compiler_params=limit(LARGE),
    )(place, counts, cols, primal, *ghosts, op_blocks)


def per_device(
    snaps_primal, snaps_adjoint, coef_primal, coef_adjoint, op_blocks, counts, col_index, ghost_send
):
    ways, space = lax.axis_size("snap"), lax.axis_size("space")
    modes = coef_primal.shape[1]
    share = modes // ways
    unknowns = snaps_primal.shape[1]
    piece = unknowns // ways
    size = op_blocks.shape[2]
    deep = space // 2
    ring = [*range(0, deep // 2, 2), *range(deep // 2 - 1, 0, -2)]
    along_z = [[h * deep + z * 2 + c for z in ring] for h in range(2) for c in range(2)]
    across_z = [[h * deep + z * 2 + c for h in range(2) for c in range(2)] for z in range(deep // 2)]
    turns = [0, 3, 4, 7, 2, 1, 6, 5]
    first_turns = [s ^ 1 for s in turns]
    around = [[p * ways + s for s in turns for p in group] for group in across_z]
    place = lax.axis_index("space").reshape(1).astype(jnp.int32)

    coef_turned = jnp.concatenate([coef_primal[:, s * share : (s + 1) * share] for s in first_turns], axis=1)
    primal_part = jnp.einsum("mr,ms->rs", coef_turned, snaps_primal, preferred_element_type=F32)
    primal_tiles = primal_part.astype(BF16).reshape(ways, share, unknowns)
    primal_tiles = exchange(primal_tiles, "snap", [first_turns])

    adjoint_part = jnp.einsum("mr,ms->rs", coef_adjoint, snaps_adjoint, preferred_element_type=F32)
    adjoint_tiles = jnp.moveaxis(adjoint_part.astype(BF16).reshape(modes, ways, piece), 1, 0)

    primal, *outgoing = sum_and_pick(place, ghost_send[0], primal_tiles, size)
    adjoint_tiles, _ = lax.optimization_barrier((adjoint_tiles, primal))
    adjoint_tiles = exchange(adjoint_tiles, "snap", [turns])
    ghosts = [swapped(o, "space", w) for o, w in zip(outgoing, space_pairings(space))]
    applied, both = applied_and_laid_out(place, counts, col_index.T, primal, ghosts, op_blocks, ways)

    both = exchange(both, "snap", [turns])
    adjoint = adjoint_tiles.astype(F32).sum(axis=0).astype(BF16)
    products = jnp.einsum("was,bs->wab", both, adjoint, preferred_element_type=F32).astype(BF16)
    rows = 2 * share // NEAR
    tiles = exchange(products.reshape(ways * NEAR, rows, modes), ("space", "snap"), around)
    total = tiles.astype(F32).sum(axis=0).astype(BF16)
    every = exchange(jnp.broadcast_to(total[None], (deep // 2, rows, modes)), "space", along_z)
    total = every.astype(F32).sum(axis=0) * (1.0 / math.sqrt(unknowns * space))
    total = exchange(jnp.broadcast_to(total[None], (NEAR, rows, modes)), "space", across_z)
    total = total.reshape(2 * share, modes)
    return (primal, applied, total[:share].T, total[share:].T)


def solution(mesh):
    placed = (
        P("snap", "space"),
        P("snap", "space"),
        P("snap", None),
        P("snap", None),
        P("space", None, None, None),
        P("space"),
        P("space", None),
        P("space", None, None),
    )
    return jax.shard_map(
        per_device,
        mesh=mesh,
        in_specs=placed,
        out_specs=(P("snap", "space"), P("snap", "space"), P(None, "snap"), P(None, "snap")),
        check_vma=False,
    )
```

```python
import math

import jax
import jax.numpy as jnp
from jax import lax
from jax.experimental import pallas as pl
from jax.experimental.pallas import tpu as pltpu
from jax.sharding import PartitionSpec as P

F32 = jnp.float32
BF16 = jnp.bfloat16
NEAR = 4
PARTS = 6
SMALL, LARGE = 12 << 20, 58 << 20


def exchange(tiles, axis, groups=None):
    return lax.all_to_all(tiles, axis, 0, 0, tiled=True, axis_index_groups=groups)


def swapped(value, axis, pairs):
    return lax.ppermute(value, axis, [(a, b) for a, b in pairs] + [(b, a) for a, b in pairs])


def space_pairings(count):
    far_odd = [(p, p + 2) for p in range(count - 2) if p % 4 >= 2]
    far_even = [(p, p + 2) for p in range(count - 2) if p % 4 < 2]
    near_odd = [(p, p + 1) for p in range(1, count - 1, 2)]
    near_even = [(p, p + 1) for p in range(0, count - 1, 2)]
    return far_odd, near_odd, far_even, near_even


def lists_of_pairings(place):
    far, near = lax.rem(place, 4) >= 2, lax.rem(place, 2) == 1
    for up, below, above in ((far, 0, 3), (near, 1, 2), (~far, 0, 3), (~near, 1, 2)):
        yield jnp.where(up, below, above), jnp.where(up, above, below)


def vmem():
    return pl.BlockSpec(memory_space=pltpu.VMEM)


def smem():
    return pl.BlockSpec(memory_space=pltpu.SMEM)


def limit(size):
    return pltpu.CompilerParams(vmem_limit_bytes=size)


def pick_kernel(place_ref, send_ref, tiles_ref, primal_ref, *out_refs):
    total = tiles_ref[0].astype(F32)
    for j in range(1, tiles_ref.shape[0]):
        total = total + tiles_ref[j].astype(F32)
    primal_ref[...] = total.astype(BF16)
    size = out_refs[0].shape[2]
    for (sent, _), out_ref in zip(lists_of_pairings(place_ref[0]), out_refs):
        for t in range(out_ref.shape[0]):
            start = pl.multiple_of(send_ref[sent, t] * size, size)
            out_ref[t] = primal_ref[:, pl.ds(start, size)]


def sum_and_pick(place, lists, tiles, size):
    _, share, unknowns = tiles.shape
    count, length = lists.shape
    return pl.pallas_call(
        pick_kernel,
        out_shape=[jax.ShapeDtypeStruct((share, unknowns), BF16)]
        + [jax.ShapeDtypeStruct((length, share, size), BF16)] * count,
        in_specs=[smem(), smem(), vmem()],
        out_specs=[vmem()] * (1 + count),
        compiler_params=limit(SMALL),
    )(place, lists, tiles)


def apply_kernel(place_ref, counts_ref, cols_ref, primal_ref, *refs):
    *ghost_refs, op_hbm, applied_ref, both_ref, held, op_ref, sems = refs
    rows, slots, size, _ = op_ref.shape
    share = primal_ref.shape[0]
    ways, _, piece = both_ref.shape
    per = piece // size
    part = rows // PARTS
    copies = []
    for i in range(PARTS):
        cut = pl.ds(i * part, part)
        copies.append(pltpu.make_async_copy(op_hbm.at[cut], op_ref.at[cut], sems.at[i]))
        copies[-1].start()
    for b in range(rows):
        held[b] = primal_ref[:, b * size : (b + 1) * size]
    for (_, received), ghost_ref in zip(lists_of_pairings(place_ref[0]), ghost_refs):
        length = ghost_ref.shape[0]
        held[pl.ds(rows + received * length, length)] = ghost_ref[...]
    for w in range(ways):
        both_ref[w, share:, :] = primal_ref[:, w * piece : (w + 1) * piece]
    for r in range(rows):
        if r % part == 0:
            copies[r // part].wait()
        blocks = []
        for k in range(slots):
            block = held[cols_ref[k, r]]
            blocks.append(jnp.where(k < counts_ref[r], block, jnp.zeros_like(block)))
        out = lax.dot_general(
            jnp.concatenate(blocks, axis=1),
            jnp.concatenate([op_ref[r, k] for k in range(slots)], axis=1),
            (((1,), (1,)), ((), ())),
            preferred_element_type=F32,
        ).astype(BF16)
        applied_ref[:, r * size : (r + 1) * size] = out
        both_ref[r // per, :share, (r % per) * size : (r % per + 1) * size] = out


def applied_and_laid_out(place, counts, cols, primal, ghosts, op_blocks, ways):
    share, unknowns = primal.shape
    rows, slots, size, _ = op_blocks.shape
    held = rows + sum(g.shape[0] for g in ghosts)
    return pl.pallas_call(
        apply_kernel,
        out_shape=[
            jax.ShapeDtypeStruct((share, unknowns), BF16),
            jax.ShapeDtypeStruct((ways, 2 * share, unknowns // ways), BF16),
        ],
        in_specs=[smem()] * 3
        + [vmem()] * (1 + len(ghosts))
        + [pl.BlockSpec(memory_space=pltpu.HBM)],
        out_specs=[vmem(), vmem()],
        scratch_shapes=[
            pltpu.VMEM((held, share, size), BF16),
            pltpu.VMEM(op_blocks.shape, BF16),
            pltpu.SemaphoreType.DMA((PARTS,)),
        ],
        compiler_params=limit(LARGE),
    )(place, counts, cols, primal, *ghosts, op_blocks)


def per_device(
    snaps_primal, snaps_adjoint, coef_primal, coef_adjoint, op_blocks, counts, col_index, ghost_send
):
    ways, space = lax.axis_size("snap"), lax.axis_size("space")
    modes = coef_primal.shape[1]
    share = modes // ways
    unknowns = snaps_primal.shape[1]
    piece = unknowns // ways
    size = op_blocks.shape[2]
    deep = space // 2
    ring = [*range(0, deep // 2, 2), *range(deep // 2 - 1, 0, -2)]
    along_z = [[h * deep + z * 2 + c for z in ring] for h in range(2) for c in range(2)]
    across_z = [[h * deep + z * 2 + c for h in range(2) for c in range(2)] for z in range(deep // 2)]
    turns = [3, 4, 7, 2, 1, 6, 5, 0]
    first_turns = [1, 2, 5, 6, 3, 0, 7, 4]
    around = [[p * ways + s for s in turns for p in group] for group in across_z]
    place = lax.axis_index("space").reshape(1).astype(jnp.int32)

    coef_turned = jnp.concatenate([coef_primal[:, s * share : (s + 1) * share] for s in first_turns], axis=1)
    primal_part = jnp.einsum("mr,ms->rs", coef_turned, snaps_primal, preferred_element_type=F32)
    primal_tiles = primal_part.astype(BF16).reshape(ways, share, unknowns)
    primal_tiles = exchange(primal_tiles, "snap", [first_turns])

    adjoint_part = jnp.einsum("mr,ms->rs", coef_adjoint, snaps_adjoint, preferred_element_type=F32)
    adjoint_tiles = jnp.moveaxis(adjoint_part.astype(BF16).reshape(modes, ways, piece), 1, 0)

    primal, *outgoing = sum_and_pick(place, ghost_send[0], primal_tiles, size)
    adjoint_tiles, _ = lax.optimization_barrier((adjoint_tiles, primal))
    adjoint_tiles = exchange(adjoint_tiles, "snap", [turns])
    ghosts = [swapped(o, "space", w) for o, w in zip(outgoing, space_pairings(space))]
    applied, both = applied_and_laid_out(place, counts, col_index.T, primal, ghosts, op_blocks, ways)

    both = exchange(both, "snap", [turns])
    adjoint = adjoint_tiles.astype(F32).sum(axis=0).astype(BF16)
    products = jnp.einsum("was,bs->wab", both, adjoint, preferred_element_type=F32).astype(BF16)
    rows = 2 * share // NEAR
    tiles = exchange(products.reshape(ways * NEAR, rows, modes), ("space", "snap"), around)
    total = tiles.astype(F32).sum(axis=0).astype(BF16)
    every = exchange(jnp.broadcast_to(total[None], (deep // 2, rows, modes)), "space", along_z)
    total = every.astype(F32).sum(axis=0) * (1.0 / math.sqrt(unknowns * space))
    total = exchange(jnp.broadcast_to(total[None], (NEAR, rows, modes)), "space", across_z)
    total = total.reshape(2 * share, modes)
    return (primal, applied, total[:share].T, total[share:].T)


def solution(mesh):
    placed = (
        P("snap", "space"),
        P("snap", "space"),
        P("snap", None),
        P("snap", None),
        P("space", None, None, None),
        P("space"),
        P("space", None),
        P("space", None, None),
    )
    return jax.shard_map(
        per_device,
        mesh=mesh,
        in_specs=placed,
        out_specs=(P("snap", "space"), P("snap", "space"), P(None, "snap"), P(None, "snap")),
        check_vma=False,
    )
```
